32 devices in a mesh: dp: 4 (over y, x), section: 2 (over core), tensor: 4 (over z).
Axes of the slice: x: 2, y: 2, z: 4, core: 2. Of those that a mesh axis runs over, the one named last changes fastest.
Arguments:
- in_delta: bfloat16 [8, 1024, 4096], P(None, ('dp', 'tensor')), may hold values from -12 to 12
- weight: bfloat16 [2, 4096, 4096], P('section', 'tensor'), may hold values from -0.09375 to 0.09375
- cache_codes: int32 [2, 2, 8, 1024, 4096], P('section', None, None, ('dp', 'tensor')), may hold values from -7 to 7, as said below
- cache_scales: float32 [2, 2, 8, 4, 32], P('section', None, None, 'dp'), may hold values from 0.2 to 6, as said below
- cotangent: bfloat16 [8, 1024, 4096], P(None, ('dp', 'tensor')), may hold values from -6 to 6
Outputs:
- out_deltas: bfloat16 [2, 8, 1024, 4096], P('section', None, ('dp', 'tensor'))
- grad_in: bfloat16 [2, 8, 1024, 4096], P('section', None, ('dp', 'tensor'))
- weight_grad: float32 [2, 4096, 4096], P('section', 'tensor', 'dp')
The draws below stay inside these ranges and needn't reach their ends.
Inputs may be any that keep to these rules, and one draw needn't show every extreme that they name: cache_codes[s, 1] equals cache_codes[s + 1, 0]: the buffer of a boundary between two segments is held by both. cache_scales[s, 1] equals cache_scales[s + 1, 0].
All inputs are finite; a program needn't handle non-finite values. Where the reference program divides by a largest or mean magnitude, that divisor is 1e-20 or more.
Results may differ from the reference program's by a relative error of at most 0.013.
Values may be sent and summed in bfloat16 or wider, within the bound.
A program may use at most 320 MiB of HBM per device.

```python
import jax
import jax.numpy as jnp
from jax import lax

D = 4096
BLOCK = 128
MBT = 256
MICRO = 8
SECTIONS = 2
BLOCKS = 32
TOKENS = 1024
N_DP = 4
N_TENSOR = 4


def boundary_codes(key):
    sub_key = jax.random.fold_in(key, 17)
    return jax.random.randint(sub_key, (SECTIONS + 1, MICRO, TOKENS, D), -7, 8, dtype=jnp.int32)


def draw_cache_codes(key, part):
    stacked = boundary_codes(key)
    return jnp.stack([stacked[:-1], stacked[1:]], axis=1)


def draw_cache_scales(key, part):
    sub_key = jax.random.fold_in(key, 29)
    shape_all = (SECTIONS + 1, MICRO, N_DP, BLOCKS)
    logs = jax.random.uniform(sub_key, shape_all, jnp.float32, jnp.log(0.5), jnp.log(4.0))
    stacked = jnp.exp(logs)
    return jnp.stack([stacked[:-1], stacked[1:]], axis=1)


def draw_in_delta(key, part):
    first_key, second_key = jax.random.split(jax.random.fold_in(key, 41), 2)
    shape_all = (MICRO, TOKENS, D)
    row_factor = jnp.exp(jax.random.uniform(second_key, (MICRO, TOKENS, 1), jnp.float32, jnp.log(0.3), jnp.log(3.0)))
    values = jax.random.normal(first_key, shape_all, jnp.float32) * row_factor
    return jnp.clip(values, -12.0, 12.0).astype(jnp.bfloat16)


def with_spikes(array, rng, source, target, blocks, factor):
    owner, partner = [(jnp.arange(array.shape[axis_at]) // (array.shape[axis_at] // blocks)).reshape([-1 if axis == axis_at else 1 for axis in range(array.ndim)]) for axis_at in (source, target)]
    chosen = jax.random.permutation(rng, blocks)[partner]
    strong = (owner == chosen) | (owner == (partner + blocks // 2) % blocks)
    return jnp.where(strong, factor * array, array)


def block_scale(rng, dims, pieces, smallest, high):
    loudness, own = 1.0, jax.random.fold_in(rng, 6)
    for axis_at, shards_of in pieces:
        steps = jnp.exp(jax.random.uniform(jax.random.fold_in(own, axis_at), (shards_of,), jnp.float32, smallest / len(pieces), high / len(pieces)))
        loudness = loudness * jnp.repeat(steps, dims[axis_at] // shards_of).reshape([-1 if axis == axis_at else 1 for axis in range(len(dims))])
    return loudness


def bell_draw(own_key, extent, scale, bound, pieces=(), held_as=jnp.bfloat16):
    values = scale * jax.random.normal(own_key, extent, jnp.float32)
    if pieces:
        values = values * block_scale(own_key, extent, pieces, -0.22, 0.18)
    return jnp.clip(values, -bound, bound).astype(held_as)


def gaussian_with(stream_key, shape, scale, reach, cuts, heavy, kind=jnp.bfloat16):
    entries = scale * jax.random.normal(stream_key, shape, jnp.float32)
    if cuts:
        entries = entries * block_scale(stream_key, shape, cuts, -0.22, 0.18)
    return jnp.clip(with_spikes(entries, jax.random.fold_in(stream_key, 3), *heavy), -reach, reach).astype(kind)


def setup_inputs(seed: int = 0) -> dict:
    splits = jax.random.split(jax.random.key(seed), 6)
    in_delta = draw_in_delta(jax.random.fold_in(splits[5], 71), 0)
    weight = bell_draw(splits[1], (SECTIONS, D, D), D ** -0.5, 0.09375, ((0, 2), (1, 4)))
    cache_codes = draw_cache_codes(jax.random.fold_in(splits[5], 71), 0)
    cache_scales = draw_cache_scales(jax.random.fold_in(splits[5], 71), 0)
    cotangent = gaussian_with(splits[4], (MICRO, TOKENS, D), 1.0, 6.0, ((1, 16),), (1, 2, 16, 2.0))
    return dict(in_delta=in_delta, weight=weight, cache_codes=cache_codes, cache_scales=cache_scales, cotangent=cotangent)


code_levels = 7.0
softness = 0.8
two_pi = 6.283185307179586
epsilon = 1e-06

def dequantize(stored_codes, scales_all):
    blocked = stored_codes.astype(jnp.float32).reshape(MICRO, N_DP, MBT, BLOCKS, BLOCK)
    return (blocked * scales_all[:, :, None, :, None] / code_levels).reshape(MICRO, TOKENS, D)

def quantize(boundary_delta):
    blocked = boundary_delta.reshape(MICRO, N_DP, MBT, BLOCKS, BLOCK)
    spread = (lax.optimization_barrier(jnp.max(jnp.abs(blocked), axis=(2, 4))) + epsilon)[:, :, None, :, None]
    level_value = code_levels * blocked / spread
    smooth = level_value - softness * jnp.sin(two_pi * level_value) / two_pi
    return (smooth * spread / code_levels).astype(jnp.bfloat16).reshape(MICRO, TOKENS, D)

def grouped_product(normed, weight_now):
    flat = normed.reshape(-1, D)
    group_width = D // N_TENSOR
    total = jnp.zeros((flat.shape[0], D), jnp.float32)
    for group in range(N_TENSOR):
        piece = jnp.dot(flat[:, group * group_width:(group + 1) * group_width], weight_now[group * group_width:(group + 1) * group_width], preferred_element_type=jnp.float32)
        total = total + lax.optimization_barrier(piece.astype(jnp.bfloat16)).astype(jnp.float32)
    return total.reshape(MICRO, TOKENS, D)

def reference(in_delta, weight, cache_codes, cache_scales, cotangent):
    incoming = in_delta
    saved_states = []
    sent_all = []
    for segment_now in range(SECTIONS):
        hidden = dequantize(cache_codes[segment_now, 0], cache_scales[segment_now, 0]) + incoming.astype(jnp.float32)
        scaling = lax.rsqrt(lax.optimization_barrier(jnp.mean(hidden * hidden, axis=-1, keepdims=True)) + epsilon)
        normed = (hidden * scaling).astype(jnp.bfloat16)
        branch = grouped_product(normed, weight[segment_now])
        boundary_delta = hidden + branch - dequantize(cache_codes[segment_now, 1], cache_scales[segment_now, 1])
        incoming = quantize(boundary_delta)
        saved_states.append((hidden, scaling, normed))
        sent_all.append(incoming)
    upstream = cotangent
    grads_in = [None] * SECTIONS
    weight_grads = [None] * SECTIONS
    for segment_now in range(SECTIONS - 1, -1, -1):
        hidden, scaling, normed = saved_states[segment_now]
        grad_raw = jnp.dot(upstream.reshape(-1, D), weight[segment_now].T, preferred_element_type=jnp.float32).reshape(MICRO, TOKENS, D)
        grad_normed = lax.optimization_barrier(grad_raw.astype(jnp.bfloat16)).astype(jnp.float32)
        normed_rep = normed.reshape(MICRO, N_DP, MBT, D)
        upstream_rep = upstream.reshape(MICRO, N_DP, MBT, D)
        total = jnp.zeros((D, D), jnp.float32)
        for replica in range(N_DP):
            partial_sum = jnp.dot(normed_rep[:, replica].reshape(-1, D).T, upstream_rep[:, replica].reshape(-1, D), preferred_element_type=jnp.float32)
            total = total + lax.optimization_barrier(partial_sum.astype(jnp.bfloat16)).astype(jnp.float32)
        unrounded = hidden * scaling
        grad_hidden = upstream.astype(jnp.float32) + scaling * (grad_normed - unrounded * lax.optimization_barrier(jnp.mean(grad_normed * unrounded, axis=-1, keepdims=True)))
        upstream = grad_hidden.astype(jnp.bfloat16)
        grads_in[segment_now] = upstream
        weight_grads[segment_now] = total
    return (jnp.stack(sent_all), jnp.stack(grads_in), jnp.stack(weight_grads))
```

```python
import jax
import jax.numpy as jnp
from jax import lax
from jax.sharding import PartitionSpec as P

code_levels = 7.0
softness = 0.8
two_pi = 6.283185307179586
epsilon = 1e-06
bf16 = jnp.bfloat16
f32 = jnp.float32
chunk_count = 1

sine_terms = (
    6.283185307179586, -41.34170224039975, 81.60524927607504, -76.70585975306136,
    42.058693944897654, -15.094642576822985, 3.8199525848482821,
)


def sine_of_turns(turns):
    rest = turns - jnp.round(turns)
    rest = jnp.where(rest > 0.25, 0.5 - rest, jnp.where(rest < -0.25, -0.5 - rest, rest))
    square = rest * rest
    total = jnp.full_like(rest, sine_terms[-1])
    for term in sine_terms[-2::-1]:
        total = total * square + term
    return total * rest


def local(in_delta, weight, cache_codes, cache_scales, cotangent):
    dp_count = lax.axis_size("dp")
    section_count = lax.axis_size("section")
    replica = lax.axis_index("dp")
    first = lax.axis_index("section") == 0
    micro_count, rows, width = in_delta.shape
    block_count = cache_scales.shape[-1]
    block = width // block_count
    part = width // dp_count
    is_power = dp_count & (dp_count - 1) == 0
    chunks = chunk_count if micro_count % chunk_count == 0 else 1
    micros = micro_count // chunks
    tokens = micros * rows

    def target(source, step):
        return source ^ step if is_power else (source + step) % dp_count

    def origin(source, step):
        return source ^ step if is_power else (source - step) % dp_count

    def exchange(value, section, step):
        pairs = [
            (source * section_count + section, target(source, step) * section_count + section)
            for source in range(dp_count)
        ]
        return lax.ppermute(value, ("dp", "section"), pairs)

    def give_back(value, section, step):
        pairs = [
            (source * section_count + section, origin(source, step) * section_count + section)
            for source in range(dp_count)
        ]
        return lax.ppermute(value, ("dp", "section"), pairs)

    def columns(value, index):
        return lax.dynamic_slice_in_dim(value, index * part, part, 1)

    weight_part = lax.all_gather(columns(weight[0], replica), "tensor", axis=0, tiled=True)

    def product(forward_here, whole, piece):
        def forward(whole, piece):
            out = jnp.dot(whole, weight_part, preferred_element_type=f32).astype(bf16)
            return out, jnp.zeros((tokens, width), bf16)

        def backward(whole, piece):
            out = lax.dot_general(
                piece, weight_part, (((1,), (1,)), ((), ())), preferred_element_type=f32
            ).astype(bf16)
            return jnp.zeros((tokens, part), bf16), out

        return lax.cond(forward_here, forward, backward, whole, piece)

    def pre(normed, upstream, forward_section):
        whole, piece = [normed], [columns(upstream, replica)]
        for step in range(1, dp_count):
            whole.append(exchange(normed, forward_section, step))
            piece.append(
                exchange(columns(upstream, target(replica, step)), 1 - forward_section, step)
            )
        return whole, piece

    def middle(whole, piece, forward_section):
        here = first if forward_section == 0 else ~first
        branch = jnp.zeros((tokens, width), bf16)
        grad = None
        order = list(range(1, dp_count)) + [0]
        for step in order:
            out, back = product(here, whole[step], piece[step])
            if step:
                out = give_back(out, forward_section, step)
                back = give_back(back, 1 - forward_section, step)
            branch = lax.dynamic_update_slice_in_dim(
                branch, out, target(replica, step) * part, 1
            )
            grad = back.astype(f32) if grad is None else grad + back.astype(f32)
        return branch, grad

    def scales_row(slot, chunk):
        now = cache_scales[0, slot, chunk * micros:(chunk + 1) * micros, 0]
        return jnp.repeat(now / code_levels, block, axis=-1)[:, None, :]

    def codes(slot, chunk):
        return cache_codes[0, slot, chunk * micros:(chunk + 1) * micros].astype(f32)

    def shaped(value):
        return value.reshape(micros, rows, width)

    def flat(value):
        return value.reshape(tokens, width)

    def rms(hidden):
        return lax.rsqrt(jnp.mean(hidden * hidden, axis=-1, keepdims=True) + epsilon)

    def finish_forward(hidden, branch, chunk):
        delta = hidden + shaped(branch).astype(f32) - codes(1, chunk) * scales_row(1, chunk)
        peak = jnp.max(jnp.abs(delta), axis=1).reshape(micros, block_count, block).max(axis=-1)
        spread = lax.pmax(peak, "tensor") + epsilon
        up_scale = jnp.repeat(code_levels / spread, block, axis=-1)[:, None, :]
        down_scale = jnp.repeat(spread / code_levels, block, axis=-1)[:, None, :]
        level = delta * up_scale
        smooth = level - (softness / two_pi) * sine_of_turns(level)
        return (smooth * down_scale).astype(bf16)

    def finish_backward(hidden, upstream, grad):
        inverse = rms(hidden)
        grad = shaped(grad.astype(bf16)).astype(f32)
        unrounded = hidden * inverse
        mean = jnp.mean(grad * unrounded, axis=-1, keepdims=True)
        return (upstream.astype(f32) + inverse * (grad - unrounded * mean)).astype(bf16)

    over = range(chunks)
    span = [slice(c * micros, (c + 1) * micros) for c in over]
    outs, grads, wholes, pieces = [None] * chunks, [None] * chunks, [], []

    with jax.named_scope("phase_a"):
        stage_a = []
        for c in over:
            hidden = codes(0, c) * scales_row(0, c) + in_delta[span[c]].astype(f32)
            normed = flat((hidden * rms(hidden)).astype(bf16))
            stage_a.append((hidden, pre(normed, flat(cotangent[span[c]]), 0)))
        stage_b = []
        for c in over:
            hidden, (whole, piece) = stage_a[c]
            branch, grad = middle(whole, piece, 0)
            outs[c] = finish_forward(hidden, branch, c)
            received = lax.ppermute(outs[c], "section", [(0, 1)])
            incoming = jnp.where(first, in_delta[span[c]], received)
            hidden = codes(0, c) * scales_row(0, c) + incoming.astype(f32)
            normed = flat((hidden * rms(hidden)).astype(bf16))
            grads[c] = finish_backward(hidden, cotangent[span[c]], grad)
            upstream = lax.ppermute(grads[c], "section", [(1, 0)])
            stage_b.append((hidden, upstream, pre(normed, flat(upstream), 1)))

    with jax.named_scope("weight_grad"):
        def gathered(pairs):
            whole = jnp.concatenate([w for p in pairs for w in p[0]], axis=0)
            piece = jnp.concatenate([g for p in pairs for g in p[1]], axis=0)
            return lax.dot_general(
                whole, piece, (((0,), (0,)), ((), ())), preferred_element_type=f32
            ).astype(bf16)

        from_a = [a[1] for a in stage_a]
        from_b = [b[2] for b in stage_b]
        partial = lax.cond(
            first,
            lambda a, b: gathered([(x[0], y[1]) for x, y in zip(a, b)]),
            lambda a, b: gathered([(y[0], x[1]) for x, y in zip(a, b)]),
            from_a,
            from_b,
        )
        weight_grad = lax.psum_scatter(
            partial, "tensor", scatter_dimension=0, tiled=True
        ).astype(f32)

    with jax.named_scope("phase_b"):
        for c in over:
            hidden, upstream, (whole, piece) = stage_b[c]
            branch, grad = middle(whole, piece, 1)
            outs[c] = jnp.where(first, outs[c], finish_forward(hidden, branch, c))
            grads[c] = jnp.where(first, finish_backward(hidden, upstream, grad), grads[c])

    def joined(values):
        return values[0] if chunks == 1 else jnp.concatenate(values, axis=0)

    return (joined(outs)[None], joined(grads)[None], weight_grad[None])


def solution(mesh):
    return jax.shard_map(
        local,
        mesh=mesh,
        in_specs=(
            P(None, ("dp", "tensor"), None),
            P("section", "tensor", None),
            P("section", None, None, ("dp", "tensor"), None),
            P("section", None, None, "dp", None),
            P(None, ("dp", "tensor"), None),
        ),
        out_specs=(
            P("section", None, ("dp", "tensor"), None),
            P("section", None, ("dp", "tensor"), None),
            P("section", "tensor", "dp"),
        ),
        check_vma=False,
    )
```

```python
import jax
import jax.numpy as jnp
from jax import lax
from jax.sharding import PartitionSpec as P

code_levels = 7.0
softness = 0.8
two_pi = 6.283185307179586
epsilon = 1e-06
bf16 = jnp.bfloat16
f32 = jnp.float32
chunk_count = 1

sine_terms = (
    6.283185307179586, -41.34170224039975, 81.60524927607504, -76.70585975306136,
    42.058693944897654, -15.094642576822985, 3.8199525848482821,
)


def sine_of_turns(turns):
    rest = turns - jnp.round(turns)
    rest = jnp.where(rest > 0.25, 0.5 - rest, jnp.where(rest < -0.25, -0.5 - rest, rest))
    square = rest * rest
    total = jnp.full_like(rest, sine_terms[-1])
    for term in sine_terms[-2::-1]:
        total = total * square + term
    return total * rest


def local(in_delta, weight, cache_codes, cache_scales, cotangent):
    dp_count = lax.axis_size("dp")
    section_count = lax.axis_size("section")
    replica = lax.axis_index("dp")
    first = lax.axis_index("section") == 0
    micro_count, rows, width = in_delta.shape
    block_count = cache_scales.shape[-1]
    block = width // block_count
    part = width // dp_count
    is_power = dp_count & (dp_count - 1) == 0
    chunks = chunk_count if micro_count % chunk_count == 0 else 1
    micros = micro_count // chunks
    tokens = micros * rows

    def target(source, step):
        return source ^ step if is_power else (source + step) % dp_count

    def origin(source, step):
        return source ^ step if is_power else (source - step) % dp_count

    def exchange(value, section, step):
        pairs = [
            (source * section_count + section, target(source, step) * section_count + section)
            for source in range(dp_count)
        ]
        return lax.ppermute(value, ("dp", "section"), pairs)

    def give_back(value, section, step):
        pairs = [
            (source * section_count + section, origin(source, step) * section_count + section)
            for source in range(dp_count)
        ]
        return lax.ppermute(value, ("dp", "section"), pairs)

    def columns(value, index):
        return lax.dynamic_slice_in_dim(value, index * part, part, 1)

    weight_part = lax.all_gather(columns(weight[0], replica), "tensor", axis=0, tiled=True)

    def product(forward_here, whole, piece):
        def forward(whole, piece):
            out = jnp.dot(whole, weight_part, preferred_element_type=f32).astype(bf16)
            return out, jnp.zeros((tokens, width), bf16)

        def backward(whole, piece):
            out = lax.dot_general(
                piece, weight_part, (((1,), (1,)), ((), ())), preferred_element_type=f32
            ).astype(bf16)
            return jnp.zeros((tokens, part), bf16), out

        return lax.cond(forward_here, forward, backward, whole, piece)

    relayed = dp_count == 4
    half = tokens // 2

    def pre(normed, upstream, forward_section):
        whole, piece = [normed], [columns(upstream, replica)]
        for step in range(1, dp_count):
            if relayed and step == 3:
                whole.append(jnp.concatenate([
                    exchange(whole[1][:half], forward_section, 2),
                    exchange(whole[2][half:], forward_section, 1),
                ], axis=0))
            else:
                whole.append(exchange(normed, forward_section, step))
            piece.append(
                exchange(columns(upstream, target(replica, step)), 1 - forward_section, step)
            )
        return whole, piece

    def middle(whole, piece, forward_section):
        here = first if forward_section == 0 else ~first
        branch = jnp.zeros((tokens, width), bf16)
        steps = list(range(1, dp_count)) + [0]
        forward_order = steps if forward_section == 0 else sorted(steps)
        backward_order = [3, 1, 2, 0] if relayed else steps
        top, bottom = [], []

        def home(value, step):
            return give_back(value, 1 - forward_section, step)

        def plus(value, other):
            return (value.astype(f32) + other.astype(f32)).astype(bf16)

        for ahead, behind in zip(forward_order, backward_order):
            out, back = product(here, whole[ahead], piece[behind])
            if ahead:
                out = give_back(out, forward_section, ahead)
            branch = lax.dynamic_update_slice_in_dim(
                branch, out, target(replica, ahead) * part, 1
            )
            upper, lower = back[:half], back[half:]
            if relayed and behind == 3:
                relay_upper, relay_lower = home(upper, 1), home(lower, 2)
                continue
            if relayed and behind == 1:
                lower = plus(lower, relay_lower)
            if relayed and behind == 2:
                upper = plus(upper, relay_upper)
            if behind:
                upper, lower = home(upper, behind), home(lower, behind)
            top.append(upper.astype(f32))
            bottom.append(lower.astype(f32))
        grad = jnp.concatenate([sum(top[1:], top[0]), sum(bottom[1:], bottom[0])], axis=0)
        return branch, grad

    def largest(value):
        count = lax.axis_size("tensor")
        if count & (count - 1):
            return lax.pmax(value, "tensor")
        step = 1
        while step < count:
            pairs = [(source, source ^ step) for source in range(count)]
            value = jnp.maximum(value, lax.ppermute(value, "tensor", pairs))
            step *= 2
        return value

    def scales_row(slot, chunk):
        now = cache_scales[0, slot, chunk * micros:(chunk + 1) * micros, 0]
        return jnp.repeat(now / code_levels, block, axis=-1)[:, None, :]

    def codes(slot, chunk):
        return cache_codes[0, slot, chunk * micros:(chunk + 1) * micros].astype(f32)

    def shaped(value):
        return value.reshape(micros, rows, width)

    def flat(value):
        return value.reshape(tokens, width)

    def rms(hidden):
        return lax.rsqrt(jnp.mean(hidden * hidden, axis=-1, keepdims=True) + epsilon)

    def finish_forward(hidden, branch, chunk):
        delta = hidden + shaped(branch).astype(f32) - codes(1, chunk) * scales_row(1, chunk)
        peak = jnp.max(jnp.abs(delta), axis=1).reshape(micros, block_count, block).max(axis=-1)
        spread = largest(peak) + epsilon
        up_scale = jnp.repeat(code_levels / spread, block, axis=-1)[:, None, :]
        down_scale = jnp.repeat(spread / code_levels, block, axis=-1)[:, None, :]
        level = delta * up_scale
        smooth = level - (softness / two_pi) * sine_of_turns(level)
        return (smooth * down_scale).astype(bf16)

    def finish_backward(hidden, upstream, grad):
        inverse = rms(hidden)
        grad = shaped(grad.astype(bf16)).astype(f32)
        unrounded = hidden * inverse
        mean = jnp.mean(grad * unrounded, axis=-1, keepdims=True)
        return (upstream.astype(f32) + inverse * (grad - unrounded * mean)).astype(bf16)

    over = range(chunks)
    span = [slice(c * micros, (c + 1) * micros) for c in over]
    outs, grads, wholes, pieces = [None] * chunks, [None] * chunks, [], []

    with jax.named_scope("phase_a"):
        stage_a = []
        for c in over:
            hidden = codes(0, c) * scales_row(0, c) + in_delta[span[c]].astype(f32)
            normed = flat((hidden * rms(hidden)).astype(bf16))
            stage_a.append((hidden, pre(normed, flat(cotangent[span[c]]), 0)))
        stage_b = []
        for c in over:
            hidden, (whole, piece) = stage_a[c]
            branch, grad = middle(whole, piece, 0)
            outs[c] = finish_forward(hidden, branch, c)
            received = lax.ppermute(outs[c], "section", [(0, 1)])
            incoming = jnp.where(first, in_delta[span[c]], received)
            hidden = codes(0, c) * scales_row(0, c) + incoming.astype(f32)
            normed = flat((hidden * rms(hidden)).astype(bf16))
            grads[c] = finish_backward(hidden, cotangent[span[c]], grad)
            upstream = lax.ppermute(grads[c], "section", [(1, 0)])
            stage_b.append((hidden, upstream, pre(normed, flat(upstream), 1)))

    with jax.named_scope("weight_grad"):
        def gathered(pairs, start):
            whole = jnp.concatenate([w for p in pairs for w in p[0]], axis=0)
            piece = jnp.concatenate(
                [g[:, start:start + slab] for p in pairs for g in p[1]], axis=0
            )
            return lax.dot_general(
                whole, piece, (((0,), (0,)), ((), ())), preferred_element_type=f32
            ).astype(bf16)

        slab = part // 2
        from_a = [a[1] for a in stage_a]
        from_b = [b[2] for b in stage_b]
        summed = []
        for start in (0, slab):
            partial = lax.cond(
                first,
                lambda a, b: gathered([(x[0], y[1]) for x, y in zip(a, b)], start),
                lambda a, b: gathered([(y[0], x[1]) for x, y in zip(a, b)], start),
                from_a,
                from_b,
            )
            summed.append(lax.psum_scatter(partial, "tensor", scatter_dimension=0, tiled=True))
        weight_grad = jnp.concatenate(summed, axis=1).astype(f32)

    with jax.named_scope("phase_b"):
        for c in over:
            hidden, upstream, (whole, piece) = stage_b[c]
            branch, grad = middle(whole, piece, 1)
            outs[c] = jnp.where(first, outs[c], finish_forward(hidden, branch, c))
            grads[c] = jnp.where(first, finish_backward(hidden, upstream, grad), grads[c])

    def joined(values):
        return values[0] if chunks == 1 else jnp.concatenate(values, axis=0)

    return (joined(outs)[None], joined(grads)[None], weight_grad[None])


def solution(mesh):
    return jax.shard_map(
        local,
        mesh=mesh,
        in_specs=(
            P(None, ("dp", "tensor"), None),
            P("section", "tensor", None),
            P("section", None, None, ("dp", "tensor"), None),
            P("section", None, None, "dp", None),
            P(None, ("dp", "tensor"), None),
        ),
        out_specs=(
            P("section", None, ("dp", "tensor"), None),
            P("section", None, ("dp", "tensor"), None),
            P("section", "tensor", "dp"),
        ),
        check_vma=False,
    )
```
